128 devices in a mesh: grp: 16 (over y_lo, x, core), blk: 8 (over y_hi, z).
Axes of the slice: x: 4, y: 4 (y_hi: 2, y_lo: 2; y = y_hi * 2 + y_lo), z: 4, core: 2. Of those that a mesh axis runs over, the one named last changes fastest.
Arguments:
- pixels: bfloat16 [32, 262144], P(None, ('grp', 'blk')), may hold values from -6 to 6
- landmark_index: int32 [1, 16384], P(None, ('grp', 'blk')), may hold values from 0 to 2047
- counts: int32 [1, 128], P(None, ('grp', 'blk')), may hold values from 64 to 128, as said below
- factor: bfloat16 [64, 16384], P(None, ('grp', 'blk')), may hold values from -6 to 6
Outputs:
- embedding: float32 [64, 262144], P(None, ('grp', 'blk'))
- log_degree: float32 [1, 262144], P(None, ('grp', 'blk'))
The draws below stay inside these ranges and needn't reach their ends.
Inputs may be any that keep to these rules, and one draw needn't show every extreme that they name: `landmark_index`: landmark slots of one device point at that device's own pixels. `counts`: some device has all 128 slots live in every draw.
All inputs are finite; a program needn't handle non-finite values.
Results may differ from the reference program's by a relative error of at most 0.0042.
Values may be sent and summed in bfloat16 or wider, within the bound.
No kernel may reach another device: no remote copies, remote signals or barrier semaphores. Data moves between devices by JAX's collectives and lax.ppermute only.
A program may use at most 64 MiB of HBM per device.

```python
import jax
import jax.numpy as jnp
from jax import lax

LAYERS = 32
EMB = 64
PIX_DEV = 2048
CAP = 128
OWNERS = 128
PIXELS = 262144
LANDMARKS = 16384


def draw_counts(key, part):
    removed = jax.random.randint(key, (1, OWNERS), 0, CAP // 2 + 1)
    values = CAP - removed
    chosen = jax.random.randint(jax.random.fold_in(key, 1), (), 0, OWNERS)
    places = jnp.arange(OWNERS)[None, :]
    return jnp.where(places == chosen, CAP, values).astype(jnp.int32)


def place_ends(entries, key, least, top_value):
    dims = entries.shape
    place = [jax.random.randint(jax.random.fold_in(key, axis), (), 0, dims[axis]) for axis in range(len(dims))]
    entries = entries.at[tuple(place)].set(least)
    longest = dims.index(max(dims))
    place[longest] = (place[longest] + 1) % dims[longest]
    return entries.at[tuple(place)].set(top_value)


def steps_of(stream_key, dims, pieces, low, top_value):
    def one(axis_at, parts):
        heights = jax.random.uniform(jax.random.fold_in(jax.random.fold_in(stream_key, 6), axis_at), (parts,), jnp.float32, low / len(pieces), top_value / len(pieces))
        return jnp.repeat(jnp.exp(heights), dims[axis_at] // parts).reshape((-1,) + (1,) * (len(dims) - axis_at - 1))

    level = one(*pieces[0])
    for cut in pieces[1:]:
        level = level * one(*cut)
    return level


def normal_values(key, shape, width, most, shards=(), kind=jnp.bfloat16):
    level = steps_of(key, shape, shards, -0.22, 0.18) if shards else 1.0
    entries = jax.random.normal(key, shape, jnp.float32) * width * level
    return jnp.minimum(jnp.maximum(entries, -most), most).astype(kind)


def setup_inputs(seed: int = 0) -> dict:
    key_of = jax.random.split(jax.random.key(seed), 5)
    return {
        "pixels": normal_values(key_of[0], (LAYERS, PIXELS), 1.0, 6.0, ((1, 128),)),
        "landmark_index": place_ends(jax.random.randint(key_of[1], (1, LANDMARKS), 0, PIX_DEV), jax.random.fold_in(key_of[1], 1), 0, PIX_DEV - 1).astype(jnp.int32),
        "counts": draw_counts(jax.random.fold_in(key_of[4], 71), 0),
        "factor": normal_values(key_of[3], (EMB, LANDMARKS), 1.0, 6.0, ((1, 128),)),
    }


def reference(pixels, landmark_index, counts, factor):
    slots = jnp.arange(OWNERS * CAP, dtype=jnp.int32)
    owner = (slots // CAP).astype(jnp.int32)
    global_index = (landmark_index[0] + owner * PIX_DEV).astype(jnp.int32)
    land = jnp.take(pixels, global_index, axis=1)
    valid = slots % CAP < jnp.take(counts[0], owner)
    pix_sq = lax.optimization_barrier(jnp.sum(jnp.square(pixels.astype(jnp.float32)), axis=0, keepdims=True))
    land_blocks = jnp.transpose(land.reshape(LAYERS, OWNERS, CAP), (1, 0, 2))
    fac_blocks = jnp.transpose(factor.reshape(EMB, OWNERS, CAP), (1, 0, 2))
    mask_blocks = valid.reshape(OWNERS, CAP)

    def absorb(carry, inputs):
        emb_sum, deg_sum = carry
        land_blk, fac_blk, mask_blk = inputs
        cross = lax.dot_general(land_blk, pixels, (((0,), (0,)), ((), ())), preferred_element_type=jnp.float32)
        land_sq = lax.optimization_barrier(jnp.sum(jnp.square(land_blk.astype(jnp.float32)), axis=0))[:, None]
        dist = land_sq + pix_sq - 2.0 * cross
        kern = jnp.where(mask_blk[:, None], jnp.exp(-(2.0 / LAYERS) * dist), 0.0).astype(jnp.bfloat16)
        emb_sum = emb_sum + jnp.dot(fac_blk, kern, preferred_element_type=jnp.float32)
        deg_sum = deg_sum + lax.optimization_barrier(jnp.sum(kern.astype(jnp.float32), axis=0, keepdims=True))
        return ((emb_sum, deg_sum), None)
    start = (jnp.zeros((EMB, OWNERS * PIX_DEV), jnp.float32), jnp.zeros((1, OWNERS * PIX_DEV), jnp.float32))
    (raw_sum, degree), _ = lax.scan(absorb, start, (land_blocks, fac_blocks, mask_blocks))
    scaled = raw_sum * lax.rsqrt(degree)
    norms = jnp.sqrt(lax.optimization_barrier(jnp.mean(scaled * scaled, axis=1, keepdims=True)) + 1e-06)
    live = jnp.sum(counts.astype(jnp.float32))
    return (scaled / norms, jnp.log(degree / live))
```

```python
import functools

import jax
import jax.numpy as jnp
import numpy as np
from jax import lax
from jax.experimental import pallas as pl
from jax.experimental.pallas import tpu as pltpu
from jax.sharding import Mesh
from jax.sharding import PartitionSpec as P

LAYERS = 32
EMB = 64
LIVE = EMB
LAND = 80
EXTRA = LAND + LAYERS
FEAT = 128
SCALE = float(np.log2(np.e) * 2.0 / LAYERS)
AXES = ("ylo", "x", "core", "yhi", "z")
CHIPS = ("ylo", "x", "yhi", "z")


def pieces(row):
    high = row.astype(jnp.bfloat16).astype(jnp.float32)
    middle = (row - high).astype(jnp.bfloat16).astype(jnp.float32)
    return high, middle, row - high - middle


def stack_rows(rows, count, width):
    at = lax.broadcasted_iota(jnp.int32, (count, width), 0)
    out = jnp.zeros((count, width), jnp.float32)
    for i, row in enumerate(rows):
        out = jnp.where(at == i, row, out)
    return out


def prepare_kernel(counts_ref, pixels_ref, index_ref, factor_ref, record_ref, pixop_ref):
    slots, width = index_ref.shape[1], pixels_ref.shape[1]
    pixels = pixels_ref[...]
    picked = lax.broadcasted_iota(jnp.int32, (width, slots), 0) == index_ref[...]
    land = jnp.dot(pixels, picked.astype(jnp.bfloat16), preferred_element_type=jnp.float32)
    land_sq = jnp.sum(land * land, axis=0, keepdims=True)
    live = lax.broadcasted_iota(jnp.int32, (1, slots), 1) < counts_ref[0, 0]
    factor = jnp.where(live, factor_ref[...].astype(jnp.float32), 0.0)
    ones = jnp.ones((1, slots), jnp.float32)
    record = jnp.concatenate(
        [
            factor,
            stack_rows([live.astype(jnp.float32)], LAND - EMB, slots),
            land,
            stack_rows([-p for p in pieces(land_sq)] + [ones] * 3, FEAT - EXTRA, slots),
        ],
        axis=0,
    )
    record_ref[...] = record.T.astype(jnp.bfloat16)
    wide = pixels.astype(jnp.float32)
    pix_sq = jnp.sum(wide * wide, axis=0, keepdims=True)
    ones = jnp.ones((1, width), jnp.float32)
    pixop_ref[:LAND, :] = jnp.zeros((LAND, width), jnp.bfloat16)
    pixop_ref[LAND:EXTRA, :] = (2.0 * wide).astype(jnp.bfloat16)
    pixop_ref[EXTRA:, :] = stack_rows(
        [ones] * 3 + [-p for p in pieces(pix_sq)], FEAT - EXTRA, width
    ).astype(jnp.bfloat16)


def prepare(pixels, landmark_index, counts, factor):
    slots, width = landmark_index.shape[1], pixels.shape[1]
    vmem = pl.BlockSpec(memory_space=pltpu.VMEM)
    return pl.pallas_call(
        prepare_kernel,
        out_shape=(
            jax.ShapeDtypeStruct((slots, FEAT), jnp.bfloat16),
            jax.ShapeDtypeStruct((FEAT, width), jnp.bfloat16),
        ),
        in_specs=[pl.BlockSpec(memory_space=pltpu.SMEM), vmem, vmem, vmem],
        out_specs=(vmem, vmem),
        name="prepare",
    )(counts, pixels, landmark_index, factor)


def accumulate_kernel(first, tile, record_ref, pixop_ref, *refs):
    sums_ref = refs[-1]
    if first:
        sums_ref[...] = jnp.zeros_like(sums_ref)
    else:
        sums_ref[...] = refs[0][...]

    def step(t, carry):
        record = record_ref[pl.ds(pl.multiple_of(t * tile, tile), tile), :]
        dist = jnp.dot(record, pixop_ref[...], preferred_element_type=jnp.float32)
        kern = jnp.exp2(dist * SCALE).astype(jnp.bfloat16)
        sums_ref[...] += jnp.dot(record.T[:LAND, :], kern, preferred_element_type=jnp.float32)
        return carry

    lax.fori_loop(0, record_ref.shape[0] // tile, step, 0)


def accumulate(records, pixop, sums=None, tile=1024):
    slots, width = records.shape[0], pixop.shape[1]
    vmem = pl.BlockSpec(memory_space=pltpu.VMEM)
    args = (records, pixop) + (() if sums is None else (sums,))
    return pl.pallas_call(
        functools.partial(accumulate_kernel, sums is None, tile),
        out_shape=jax.ShapeDtypeStruct((LAND, width), jnp.float32),
        in_specs=[vmem] * len(args),
        out_specs=vmem,
        input_output_aliases={} if sums is None else {2: 0},
        cost_estimate=pl.CostEstimate(
            flops=2 * slots * width * 256,
            bytes_accessed=2 * slots * FEAT,
            transcendentals=slots * width,
        ),
        compiler_params=pltpu.CompilerParams(vmem_limit_bytes=48 << 20),
        name="accumulate",
    )(*args)


def scale_kernel(counts_ref, sums_ref, scaled_ref, total_ref):
    scaled = sums_ref[:EMB, :] * lax.rsqrt(sums_ref[LIVE : LIVE + 1, :])
    scaled_ref[...] = scaled
    squares = jnp.sum(scaled * scaled, axis=1, keepdims=True)
    row = jnp.broadcast_to(squares, (EMB, FEAT)).T[:1, :]
    live = jnp.full((1, FEAT - EMB), counts_ref[0, 0].astype(jnp.float32))
    total_ref[...] = jnp.concatenate([row, live], axis=1)


def scale(counts, sums):
    vmem = pl.BlockSpec(memory_space=pltpu.VMEM)
    return pl.pallas_call(
        scale_kernel,
        out_shape=(
            jax.ShapeDtypeStruct((EMB, sums.shape[1]), jnp.float32),
            jax.ShapeDtypeStruct((1, FEAT), jnp.float32),
        ),
        in_specs=[pl.BlockSpec(memory_space=pltpu.SMEM), vmem],
        out_specs=(vmem, vmem),
        name="scale",
    )(counts, sums)


def finish_kernel(pixel_count, totals_ref, scaled_ref, sums_ref, embedding_ref, log_ref):
    total = jnp.sum(totals_ref[...], axis=0, keepdims=True)
    live = jnp.sum(total[:, LIVE : LIVE + 1])
    norms = jnp.sqrt(jnp.broadcast_to(total, (FEAT, FEAT)).T[:EMB, :1] / pixel_count + 1e-06)
    embedding_ref[...] = scaled_ref[...] * (1.0 / norms)
    log_ref[...] = jnp.log(sums_ref[LIVE : LIVE + 1, :] / live)


def finish(totals, scaled, sums):
    width = scaled.shape[1]
    vmem = pl.BlockSpec(memory_space=pltpu.VMEM)
    return pl.pallas_call(
        functools.partial(finish_kernel, float(width * totals.shape[0])),
        out_shape=(
            jax.ShapeDtypeStruct((EMB, width), jnp.float32),
            jax.ShapeDtypeStruct((1, width), jnp.float32),
        ),
        in_specs=[vmem] * 3,
        out_specs=(vmem, vmem),
        name="finish",
    )(totals, scaled, sums)


def to_all(x, axes):
    copies = jnp.broadcast_to(x[None], (lax.axis_size(axes),) + x.shape)
    return lax.all_to_all(copies, axes, 0, 0, tiled=True)


def per_device(pixels, landmark_index, counts, factor):
    record, pixop = prepare(pixels, landmark_index, counts, factor)
    records = to_all(record, CHIPS).reshape(-1, FEAT)
    others = lax.ppermute(records, "core", [(0, 1), (1, 0)])
    sums = accumulate(records, pixop)
    sums = accumulate(others, pixop, sums)
    scaled, total = scale(counts, sums)
    totals = to_all(total[0], AXES)
    return finish(totals, scaled, sums)


def solution(mesh):
    fine = Mesh(mesh.devices.reshape(2, 4, 2, 2, 4), AXES)
    placed = P(None, AXES)
    return jax.shard_map(
        per_device,
        mesh=fine,
        in_specs=(placed,) * 4,
        out_specs=(placed, placed),
        check_vma=False,
    )
```

```python
import functools

import jax
import jax.numpy as jnp
import numpy as np
from jax import lax
from jax.experimental import pallas as pl
from jax.experimental.pallas import tpu as pltpu
from jax.sharding import Mesh
from jax.sharding import PartitionSpec as P

LAYERS = 32
EMB = 64
LIVE = EMB
LAND = 80
EXTRA = LAND + LAYERS
FEAT = 128
SCALE = float(np.log2(np.e) * 2.0 / LAYERS)
AXES = ("ylo", "x", "core", "yhi", "z")
SIZES = (2, 4, 2, 2, 4)
CAP = 128
COUNT = EXTRA + 6
GRAIN = 16
BIG = 1024
SMALL = 256


def pieces(row):
    high = row.astype(jnp.bfloat16).astype(jnp.float32)
    middle = (row - high).astype(jnp.bfloat16).astype(jnp.float32)
    return high, middle, row - high - middle


def stack_rows(rows, count, width):
    at = lax.broadcasted_iota(jnp.int32, (count, width), 0)
    out = jnp.zeros((count, width), jnp.float32)
    for i, row in enumerate(rows):
        out = jnp.where(at == i, row, out)
    return out


def record_kernel(counts_ref, pixels_ref, index_ref, factor_ref, record_ref):
    slots, width = index_ref.shape[1], pixels_ref.shape[1]
    picked = lax.broadcasted_iota(jnp.int32, (width, slots), 0) == index_ref[...]
    land = jnp.dot(
        pixels_ref[...], picked.astype(jnp.bfloat16), preferred_element_type=jnp.float32
    )
    land_sq = jnp.sum(land * land, axis=0, keepdims=True)
    live = lax.broadcasted_iota(jnp.int32, (1, slots), 1) < counts_ref[0, 0]
    factor = jnp.where(live, factor_ref[...].astype(jnp.float32), 0.0)
    ones = jnp.ones((1, slots), jnp.float32)
    count = ones * counts_ref[0, 0].astype(jnp.float32)
    record = jnp.concatenate(
        [
            factor,
            stack_rows([live.astype(jnp.float32)], LAND - EMB, slots),
            land,
            stack_rows([-p for p in pieces(land_sq)] + [ones] * 3 + [count], FEAT - EXTRA, slots),
        ],
        axis=0,
    )
    record_ref[...] = record.T.astype(jnp.bfloat16)


def make_record(pixels, landmark_index, counts, factor):
    vmem = pl.BlockSpec(memory_space=pltpu.VMEM)
    return pl.pallas_call(
        record_kernel,
        out_shape=jax.ShapeDtypeStruct((landmark_index.shape[1], FEAT), jnp.bfloat16),
        in_specs=[pl.BlockSpec(memory_space=pltpu.SMEM), vmem, vmem, vmem],
        out_specs=vmem,
        compiler_params=pltpu.CompilerParams(vmem_limit_bytes=16 << 20),
        name="record",
    )(counts, pixels, landmark_index, factor)


def operand_kernel(pixels_ref, pixop_ref):
    width = pixels_ref.shape[1]
    wide = pixels_ref[...].astype(jnp.float32)
    pix_sq = jnp.sum(wide * wide, axis=0, keepdims=True)
    ones = jnp.ones((1, width), jnp.float32)
    pixop_ref[:LAND, :] = jnp.zeros((LAND, width), jnp.bfloat16)
    pixop_ref[LAND:EXTRA, :] = (2.0 * wide).astype(jnp.bfloat16)
    pixop_ref[EXTRA:, :] = stack_rows(
        [ones] * 3 + [-p for p in pieces(pix_sq)], FEAT - EXTRA, width
    ).astype(jnp.bfloat16)


def make_operand(pixels):
    vmem = pl.BlockSpec(memory_space=pltpu.VMEM)
    return pl.pallas_call(
        operand_kernel,
        out_shape=jax.ShapeDtypeStruct((FEAT, pixels.shape[1]), jnp.bfloat16),
        in_specs=[vmem],
        out_specs=vmem,
        cost_estimate=pl.CostEstimate(
            flops=pixels.size * 8, bytes_accessed=pixels.size * 10, transcendentals=0
        ),
        compiler_params=pltpu.CompilerParams(vmem_limit_bytes=16 << 20),
        name="operand",
    )(pixels)


def accumulate_kernel(n_records, n_sides, first, *refs):
    record_refs, refs = refs[:n_records], refs[n_records:]
    pixop_refs, refs = refs[:n_sides], refs[n_sides:]
    packed_ref = refs[-1]
    sums_refs = refs[-1 - n_sides : -1]
    for i, sums_ref in enumerate(sums_refs):
        sums_ref[...] = jnp.zeros_like(sums_ref) if first else refs[i][...]

    rows = lax.broadcasted_iota(jnp.int32, (GRAIN, FEAT), 0)
    lanes = lax.broadcasted_iota(jnp.int32, (GRAIN, FEAT), 1)
    at_count = (rows == 0) & (lanes == COUNT)
    filled = jnp.int32(0)
    for record_ref in record_refs:
        for start in range(0, record_ref.shape[0], CAP):
            head = record_ref[start : start + GRAIN, :].astype(jnp.float32)
            count = jnp.sum(jnp.where(at_count, head, 0.0)).astype(jnp.int32)
            packed_ref[pl.ds(pl.multiple_of(filled, GRAIN), CAP), :] = record_ref[
                start : start + CAP, :
            ]
            filled += (count + (GRAIN - 1)) // GRAIN * GRAIN
    packed_ref[pl.ds(pl.multiple_of(filled, GRAIN), SMALL), :] = jnp.zeros(
        (SMALL, FEAT), jnp.bfloat16
    )

    def add(start, size):
        record = packed_ref[pl.ds(pl.multiple_of(start, SMALL), size), :]
        columns = record.T[:LAND, :]
        for pixop_ref, sums_ref in zip(pixop_refs, sums_refs, strict=True):
            dist = jnp.dot(record, pixop_ref[...], preferred_element_type=jnp.float32)
            kern = jnp.exp2(dist * SCALE).astype(jnp.bfloat16)
            sums_ref[...] += jnp.dot(columns, kern, preferred_element_type=jnp.float32)

    big = filled // BIG
    small = (filled - big * BIG + (SMALL - 1)) // SMALL
    lax.fori_loop(0, big, lambda t, c: (add(t * BIG, BIG), c)[1], 0)
    lax.fori_loop(0, small, lambda t, c: (add(big * BIG + t * SMALL, SMALL), c)[1], 0)


def accumulate(records, pixops, sums=()):
    slots, width, sides = sum(r.shape[0] for r in records), pixops[0].shape[1], len(pixops)
    vmem = pl.BlockSpec(memory_space=pltpu.VMEM)
    args = (*records, *pixops, *sums)
    return pl.pallas_call(
        functools.partial(accumulate_kernel, len(records), sides, not sums),
        out_shape=(jax.ShapeDtypeStruct((LAND, width), jnp.float32),) * sides,
        in_specs=[vmem] * len(args),
        out_specs=(vmem,) * sides,
        scratch_shapes=[pltpu.VMEM((slots + BIG, FEAT), jnp.bfloat16)],
        input_output_aliases={len(records) + sides + i: i for i in range(len(sums))},
        cost_estimate=pl.CostEstimate(
            flops=2 * slots * width * sides * 256,
            bytes_accessed=2 * slots * FEAT,
            transcendentals=slots * width * sides,
        ),
        compiler_params=pltpu.CompilerParams(vmem_limit_bytes=48 << 20),
        name="accumulate",
    )(*args)


def scale_kernel(counts_ref, mine_ref, theirs_ref, scaled_ref, degree_ref, total_ref):
    degree = mine_ref[LIVE : LIVE + 1, :] + theirs_ref[LIVE : LIVE + 1, :]
    degree_ref[...] = degree
    scaled = (mine_ref[:EMB, :] + theirs_ref[:EMB, :]) * lax.rsqrt(degree)
    scaled_ref[...] = scaled
    squares = jnp.sum(scaled * scaled, axis=1, keepdims=True)
    row = jnp.broadcast_to(squares, (EMB, FEAT)).T[:1, :]
    live = jnp.full((1, FEAT - EMB), counts_ref[0, 0].astype(jnp.float32))
    total_ref[...] = jnp.concatenate([row, live], axis=1)


def scale(counts, mine, theirs):
    width = mine.shape[1]
    vmem = pl.BlockSpec(memory_space=pltpu.VMEM)
    return pl.pallas_call(
        scale_kernel,
        out_shape=(
            jax.ShapeDtypeStruct((EMB, width), jnp.float32),
            jax.ShapeDtypeStruct((1, width), jnp.float32),
            jax.ShapeDtypeStruct((1, FEAT), jnp.float32),
        ),
        in_specs=[pl.BlockSpec(memory_space=pltpu.SMEM), vmem, vmem],
        out_specs=(vmem, vmem, vmem),
        compiler_params=pltpu.CompilerParams(vmem_limit_bytes=16 << 20),
        name="scale",
    )(counts, mine, theirs)


def finish_kernel(pixel_count, totals_ref, scaled_ref, degree_ref, embedding_ref, log_ref):
    total = jnp.sum(totals_ref[...], axis=0, keepdims=True)
    live = jnp.sum(total[:, LIVE : LIVE + 1])
    norms = jnp.sqrt(jnp.broadcast_to(total, (FEAT, FEAT)).T[:EMB, :1] / pixel_count + 1e-06)
    embedding_ref[...] = scaled_ref[...] * (1.0 / norms)
    log_ref[...] = jnp.log(degree_ref[...] / live)


def finish(totals, scaled, degree):
    width = scaled.shape[1]
    vmem = pl.BlockSpec(memory_space=pltpu.VMEM)
    return pl.pallas_call(
        functools.partial(finish_kernel, float(width * totals.shape[0])),
        out_shape=(
            jax.ShapeDtypeStruct((EMB, width), jnp.float32),
            jax.ShapeDtypeStruct((1, width), jnp.float32),
        ),
        in_specs=[vmem] * 3,
        out_specs=(vmem, vmem),
        compiler_params=pltpu.CompilerParams(vmem_limit_bytes=16 << 20),
        name="finish",
    )(totals, scaled, degree)


def to_all(x, axes):
    copies = jnp.broadcast_to(x[None], (lax.axis_size(axes),) + x.shape)
    return lax.all_to_all(copies, axes, 0, 0, tiled=True)


def moved(move):
    pairs = []
    for i in range(int(np.prod(SIZES))):
        ylo, x, core, yhi, z = (int(v) for v in np.unravel_index(i, SIZES))
        to = move({"x": x, "y": 2 * yhi + ylo, "z": z, "core": core})
        place = (to["y"] % 2, to["x"], to["core"], to["y"] // 2, to["z"])
        pairs.append((i, int(np.ravel_multi_index(place, SIZES))))
    return pairs


def along(axes, hops):
    def move(at):
        axis = axes[at["core"]]
        return {**at, axis: (at[axis] + hops) % 4}

    return moved(move)


def per_device(pixels, landmark_index, counts, factor):
    swap = moved(lambda at: {**at, "core": 1 - at["core"]})
    record = make_record(pixels, landmark_index, counts, factor)
    pixops = [make_operand(pixels), make_operand(lax.ppermute(pixels, AXES, swap))]
    gathered = record
    for axes in (("x", "y"), ("y", "z")):
        far, up, down = (lax.ppermute(gathered, AXES, along(axes, h)) for h in (2, 1, 3))
        gathered = jnp.concatenate([gathered, up, down, far], axis=0)
    last = ("z", "x")
    up = lax.ppermute(gathered, AXES, along(last, 1))
    down = lax.ppermute(gathered, AXES, along(last, 3))
    sums = accumulate([gathered], pixops)
    gathered, up, down = lax.optimization_barrier((gathered, up, down))
    far = lax.ppermute(gathered, AXES, along(last, 2))
    mine, theirs = accumulate([up, down], pixops, sums)
    (theirs,) = accumulate([far], pixops[1:], (theirs,))
    swapped = lax.ppermute(theirs, AXES, swap)
    (mine,) = accumulate([far], pixops[:1], (mine,))
    scaled, degree, total = scale(counts, mine, swapped)
    totals = to_all(total[0], AXES)
    return finish(totals, scaled, degree)


def solution(mesh):
    fine = Mesh(mesh.devices.reshape(SIZES), AXES)
    placed = P(None, AXES)
    return jax.shard_map(
        per_device,
        mesh=fine,
        in_specs=(placed,) * 4,
        out_specs=(placed, placed),
        check_vma=False,
    )
```
